32 devices in a mesh: dp: 32 (over z, y, x, core).
Axes of the slice: x: 2, y: 2, z: 4, core: 2. Of those that a mesh axis runs over, the one named last changes fastest.
Arguments:
- tokens: bfloat16 [8192, 896], P('dp'), may hold values from -6 to 6
- doc_ids: int32 [8192], P('dp'), may hold values from 0 to 15, as said below
- norm_gains: bfloat16 [2, 896], P(None, 'dp'), may hold values from 0.5 to 1.5
- w_qkv: bfloat16 [896, 1152], P('dp'), may hold values from -0.1875 to 0.1875
- b_qkv: bfloat16 [1152], P('dp'), may hold values from -1.5 to 1.5
- w_out: bfloat16 [896, 896], P('dp'), may hold values from -0.75 to 0.75
- w_gate: bfloat16 [896, 4864], P('dp'), may hold values from -0.1875 to 0.1875
- w_up: bfloat16 [896, 4864], P('dp'), may hold values from -0.1875 to 0.1875
- w_down: bfloat16 [4864, 896], P('dp'), may hold values from -0.078125 to 0.078125
- cotangent: bfloat16 [8192, 896], P('dp'), may hold values from -6 to 6
Outputs:
- activations: bfloat16 [8192, 896], P('dp')
- input_grad: float32 [8192, 896], P('dp')
- grad_gains: float32 [2, 896], P(None, 'dp')
- grad_qkv: float32 [896, 1152], P('dp')
- grad_bias: float32 [1152], P('dp')
- grad_out: float32 [896, 896], P('dp')
- grad_gate: float32 [896, 4864], P('dp')
- grad_up: float32 [896, 4864], P('dp')
- grad_down: float32 [4864, 896], P('dp')
The draws below stay inside these ranges and needn't reach their ends.
Inputs may be any that keep to these rules, and one draw needn't show every extreme that they name: `doc_ids`: on each device's 256 tokens the document numbers start at 0 and rise by 0 or 1 from one token to the next, up to max(16, 2) - 1; a document lies on one device; in every draw some device holds a single document of 256 tokens and some device reaches the largest document number.
All inputs are finite; a program needn't handle non-finite values.
Results may differ from the reference program's by a relative error of at most 0.011.
Values may be sent and summed in bfloat16 or wider, within the bound.
No kernel may reach another device: no remote copies, remote signals or barrier semaphores. Data moves between devices by JAX's collectives and lax.ppermute only.
A program may use at most 256 MiB of HBM per device.

```python
import jax
import jax.numpy as jnp
from jax import lax

HEADS = 14
KV_HEADS = 2
HEAD_DIM = 64
FF = 4864
TOK_DEV = 256
D = 896
QKV = 1152
TOKENS = 8192


def draw_doc_ids(key, part):
    device_rows = TOKENS // TOK_DEV
    doc_most = max(TOK_DEV // 16, 2)
    period = TOK_DEV // doc_most
    key_rate, key_cuts, key_lone = jax.random.split(key, 3)
    exponent = jax.random.randint(key_rate, (device_rows, 1), 6, 11)
    spacing = jnp.left_shift(jnp.ones_like(exponent), exponent)
    raw_draws = jax.random.randint(key_cuts, (device_rows, TOK_DEV), 0, 1 << 30)
    cut_marks = (raw_draws % spacing == 0).astype(jnp.int32)
    column = jnp.arange(TOK_DEV, dtype=jnp.int32)[None, :]
    row_index = jnp.arange(device_rows, dtype=jnp.int32)[:, None]
    lone_row = jax.random.randint(key_lone, (), 0, device_rows)
    dense_row = (lone_row + 1) % device_rows
    regular_cuts = (column % period == 0).astype(jnp.int32)
    cut_marks = jnp.where(row_index == dense_row, regular_cuts, cut_marks)
    cut_marks = jnp.where((column == 0) | (row_index == lone_row), 0, cut_marks)
    counted = jnp.cumsum(cut_marks, axis=1)
    return jnp.minimum(counted, doc_most - 1).astype(jnp.int32).reshape(TOKENS)


def draw_b_qkv(key, part):
    key_base = jax.random.fold_in(key, 0)
    base_vals = jnp.clip(0.5 * jax.random.normal(key_base, (QKV,), dtype=jnp.float32), -1.5, 1.5)
    return base_vals.astype(jnp.bfloat16)


def shard_levels(stream_key, extent, cuts, low, largest):
    def one(axis_at, shards_of):
        heights = jax.random.uniform(jax.random.fold_in(jax.random.fold_in(stream_key, 6), axis_at), (shards_of,), jnp.float32, low / len(cuts), largest / len(cuts))
        return jnp.repeat(jnp.exp(heights), extent[axis_at] // shards_of).reshape((-1,) + (1,) * (len(extent) - axis_at - 1))

    level = one(*cuts[0])
    for cut in cuts[1:]:
        level = level * one(*cut)
    return level


def normal_values(stream_key, shape, width, most, shards=(), held_as=jnp.bfloat16):
    level = shard_levels(stream_key, shape, shards, -0.22, 0.18) if shards else 1.0
    entries = jax.random.normal(stream_key, shape, jnp.float32) * width * level
    return jnp.minimum(jnp.maximum(entries, -most), most).astype(held_as)


def setup_inputs(seed: int = 0) -> dict:
    keys = jax.random.split(jax.random.key(seed), 11)
    tokens = normal_values(keys[0], (TOKENS, D), 1.0, 6.0, ((0, 32),))
    doc_ids = draw_doc_ids(jax.random.fold_in(keys[10], 71), 0)
    norm_gains = jnp.clip(1.0 + 0.1 * jax.random.normal(keys[2], (2, D), jnp.float32), 0.5, 1.5).astype(jnp.bfloat16)
    w_qkv = normal_values(keys[3], (D, QKV), D ** -0.5, 0.1875, ((0, 32),))
    b_qkv = draw_b_qkv(jax.random.fold_in(keys[10], 71), 0)
    w_out = normal_values(keys[5], (D, D), (D // 16) ** -0.5, 0.75, ((0, 32),))
    w_gate = normal_values(keys[6], (D, FF), D ** -0.5, 0.1875, ((0, 32),))
    w_up = normal_values(keys[7], (D, FF), D ** -0.5, 0.1875, ((0, 32),))
    w_down = normal_values(keys[8], (FF, D), FF ** -0.5, 0.078125, ((0, 32),))
    cotangent = normal_values(keys[9], (TOKENS, D), 1.0, 6.0, ((0, 32),))
    return {"tokens": tokens, "doc_ids": doc_ids, "norm_gains": norm_gains, "w_qkv": w_qkv, "b_qkv": b_qkv, "w_out": w_out, "w_gate": w_gate, "w_up": w_up, "w_down": w_down, "cotangent": cotangent}


ROPE_BASE = 1000000.0
NORM_EPS = 1e-06

@jax.custom_vjp
def low(v):
    return lax.optimization_barrier(v.astype(jnp.bfloat16)).astype(jnp.float32)

@jax.custom_vjp
def low_back(v):
    return v

def low_keep(v):
    return (low(v), None)

def low_pass(kept, grad):
    return (grad,)

def back_keep(v):
    return (v, None)

def back_low(kept, grad):
    return (low(grad),)
low.defvjp(low_keep, low_pass)
low_back.defvjp(back_keep, back_low)

def rope_tables(doc_row, head_size):
    tok_rows = doc_row.shape[0]
    positions_idx = jnp.arange(tok_rows, dtype=jnp.int32)
    earlier = jnp.concatenate([doc_row[:1], doc_row[:-1]])
    starts = lax.cummax(jnp.where(doc_row != earlier, positions_idx, 0), axis=0)
    position = (positions_idx - starts).astype(jnp.float32)
    half_size = head_size // 2
    inverse = ROPE_BASE ** (-(jnp.arange(half_size, dtype=jnp.float32) * 2.0 / head_size))
    angles = position[:, None] * inverse[None, :]
    cosine_full = jnp.concatenate([jnp.cos(angles), jnp.cos(angles)], axis=-1)
    sine_full = jnp.concatenate([jnp.sin(angles), jnp.sin(angles)], axis=-1)
    return (cosine_full, sine_full)

def rotate_half(values):
    half_size = values.shape[-1] // 2
    return jnp.concatenate([-values[..., half_size:], values[..., :half_size]], axis=-1)

def rotate(values, cosine_full, sine_full):
    return values * cosine_full[:, None, :] + rotate_half(values) * sine_full[:, None, :]

def normalize(values):
    return values * lax.rsqrt(lax.optimization_barrier(jnp.mean(values * values, axis=-1, keepdims=True)) + NORM_EPS)

def matmul(left, right):
    return jnp.dot(left, right, precision=lax.Precision.HIGHEST, preferred_element_type=jnp.float32)

def block_forward(norm_gains, w_qkv, b_qkv, w_out, w_gate, w_up, w_down, hidden_in, doc_row):
    tok_rows = hidden_in.shape[0]
    kv_width = KV_HEADS * HEAD_DIM
    group_size = HEADS // KV_HEADS
    cosine_full, sine_full = rope_tables(doc_row, HEAD_DIM)
    normed_one = low(normalize(hidden_in) * norm_gains[0])
    projected = low_back(matmul(normed_one, w_qkv) + b_qkv)
    queries = projected[:, :D].reshape(tok_rows, HEADS, HEAD_DIM)
    keys_raw = projected[:, D:D + kv_width].reshape(tok_rows, KV_HEADS, HEAD_DIM)
    values = projected[:, D + kv_width:].reshape(tok_rows, KV_HEADS, HEAD_DIM)
    queries = low(rotate(queries, cosine_full, sine_full) * 0.125)
    keys_rot = low(rotate(keys_raw, cosine_full, sine_full))
    values = low(values)
    queries = queries.reshape(tok_rows, KV_HEADS, group_size, HEAD_DIM)
    scores = jnp.einsum('qcgd,kcd->cgqk', queries, keys_rot, precision=lax.Precision.HIGHEST)
    scores = low_back(scores)
    row_ids = jnp.arange(tok_rows, dtype=jnp.int32)
    allowed = (doc_row[:, None] == doc_row[None, :]) & (row_ids[None, :] <= row_ids[:, None])
    scores = jnp.where(allowed[None, None], scores, -jnp.inf)
    prob_rows = low(jax.nn.softmax(scores, axis=-1))
    attended = jnp.einsum('cgqk,kcd->qcgd', prob_rows, values, precision=lax.Precision.HIGHEST)
    attended = low(low_back(attended.reshape(tok_rows, D)))
    middle = hidden_in + low_back(matmul(attended, w_out))
    normed_two = low(normalize(middle) * norm_gains[1])
    gate_val = low_back(matmul(normed_two, w_gate))
    up_val = low_back(matmul(normed_two, w_up))
    hidden_act = low(jax.nn.silu(gate_val) * up_val)
    return middle + low_back(matmul(hidden_act, w_down))

def reference(tokens, doc_ids, norm_gains, w_qkv, b_qkv, w_out, w_gate, w_up, w_down, cotangent):
    params = tuple((item.astype(jnp.float32) for item in (norm_gains, w_qkv, b_qkv, w_out, w_gate, w_up, w_down)))
    device_rows = TOKENS // TOK_DEV
    inputs_rows = tokens.astype(jnp.float32).reshape(device_rows, TOK_DEV, D)
    cot_rows = cotangent.astype(jnp.float32).reshape(device_rows, TOK_DEV, D)
    doc_rows = doc_ids.astype(jnp.int32).reshape(device_rows, TOK_DEV)

    def scan_step(totals, item):
        hidden_in, doc_row, cot_row = item

        def forward_fn(weights, hidden_now):
            return block_forward(*weights, hidden_now, doc_row)
        result, pullback = jax.vjp(forward_fn, params, hidden_in)
        weight_grads, input_part = pullback(cot_row)
        totals = jax.tree.map(lambda left, right: left + right, totals, weight_grads)
        return (totals, (result.astype(jnp.bfloat16), input_part))
    zeros_init = jax.tree.map(lambda item: jnp.zeros_like(item, dtype=jnp.float32), params)
    totals, (results, input_parts) = lax.scan(scan_step, zeros_init, (inputs_rows, doc_rows, cot_rows))
    return (results.reshape(TOKENS, D), input_parts.reshape(TOKENS, D), totals[0], totals[1], totals[2], totals[3], totals[4], totals[5], totals[6])
```

```python
import itertools
import math

import jax
import jax.numpy as jnp
from jax import lax
from jax.sharding import PartitionSpec as P

HEAD_DIM = 64
ROPE_BASE = 1000000.0
NORM_EPS = 1e-06
BF = jnp.bfloat16
F32 = jnp.float32


class Grid:
    def __init__(self, n):
        chips = n // 2
        self.n = n
        self.A = 4 if chips % 4 == 0 else 1
        rest = chips // self.A
        self.B = math.isqrt(rest)
        while rest % self.B:
            self.B -= 1
        self.C = rest // self.B
        self.T = rest * 2
        self.planes = [[a * self.T + t for t in range(self.T)] for a in range(self.A)]
        self.offsets = list(itertools.product(range(self.B), range(self.C)))

    def perm(self, da=0, db=0, dc=0, flip=0):
        pairs = []
        for a, b, c, k in itertools.product(range(self.A), range(self.B), range(self.C), range(2)):
            src = ((a * self.B + b) * self.C + c) * 2 + k
            ta, tb, tc = (a + da) % self.A, (b + db) % self.B, (c + dc) % self.C
            pairs.append((src, ((ta * self.B + tb) * self.C + tc) * 2 + (k ^ flip)))
        return pairs

    def send(self, x, **shift):
        return lax.ppermute(x, "dp", self.perm(**shift))


def dot(left, right, dims=((1,), (0,)), out=F32):
    return lax.dot_general(left, right, (dims, ((), ())), preferred_element_type=out)


def rows_dot(left, right):
    return dot(left, right, ((0,), (0,)))


def against(left, right):
    return dot(left, right, ((1,), (1,)))


def gather_all(grid, x):
    line = [x] + [grid.send(x, da=j) for j in range(1, grid.A)]
    line = jnp.concatenate([item[None] for item in line], axis=0)
    own, other = [], []
    for db, dc in grid.offsets:
        piece = line if db == dc == 0 else grid.send(line, db=db, dc=dc)
        own.append(piece[None])
        other.append(grid.send(piece, flip=1)[None])
    full = jnp.concatenate(own + other, axis=0)
    return full.reshape((grid.n,) + x.shape)


def scatter_all(grid, full):
    planes = len(grid.offsets)
    full = full.reshape((2, planes, grid.A) + full.shape[1:])
    got = grid.send(full[1].astype(BF), flip=1)
    half = full[0] + got.astype(F32)
    total = half[0]
    for index, (db, dc) in enumerate(grid.offsets):
        if index:
            total = total + grid.send(half[index].astype(BF), db=-db, dc=-dc).astype(F32)
    out = total[0]
    for j in range(1, grid.A):
        out = out + grid.send(total[j].astype(BF), da=-j).astype(F32)
    return out


def line_gather(grid, x, place):
    whole = jnp.zeros((grid.A,) + x.shape, x.dtype)
    whole = lax.dynamic_update_index_in_dim(whole, x, place, 0)
    now = x
    for j in range(1, grid.A):
        now = grid.send(now, da=1)
        whole = lax.dynamic_update_index_in_dim(whole, now, (place - j) % grid.A, 0)
    return whole


def line_scatter(grid, partial, place):
    acc = None
    for s in range(1, grid.A):
        mine = lax.dynamic_index_in_dim(partial, (place - s) % grid.A, 0, keepdims=False)
        acc = mine if acc is None else mine + acc.astype(F32)
        acc = grid.send(acc.astype(BF), da=1)
    mine = lax.dynamic_index_in_dim(partial, place, 0, keepdims=False)
    return mine if acc is None else mine + acc.astype(F32)


def plane_gather(grid, x):
    blocks = []
    for db, dc in grid.offsets:
        piece = x if db == dc == 0 else grid.send(x, db=db, dc=dc)
        blocks += [piece, grid.send(piece, flip=1)]
    return jnp.concatenate(blocks, axis=0)


def plane_scatter(grid, partial, rows):
    partial = partial.reshape(len(grid.offsets), 2, rows, partial.shape[1])
    got = grid.send(partial[:, 1].astype(BF), flip=1)
    half = partial[:, 0] + got.astype(F32)
    total = half[0]
    for index, (db, dc) in enumerate(grid.offsets):
        if index:
            total = total + grid.send(half[index].astype(BF), db=-db, dc=-dc).astype(F32)
    return total


def plane_exchange(grid, x):
    return lax.all_to_all(x, "dp", 0, 0, tiled=True, axis_index_groups=grid.planes)


def rope_tables(doc_row, head_size):
    tok_rows = doc_row.shape[0]
    positions_idx = jnp.arange(tok_rows, dtype=jnp.int32)
    earlier = jnp.concatenate([doc_row[:1], doc_row[:-1]])
    starts = lax.cummax(jnp.where(doc_row != earlier, positions_idx, 0), axis=0)
    position = (positions_idx - starts).astype(jnp.float32)
    half_size = head_size // 2
    inverse = ROPE_BASE ** (-(jnp.arange(half_size, dtype=jnp.float32) * 2.0 / head_size))
    angles = position[:, None] * inverse[None, :]
    cosine_full = jnp.concatenate([jnp.cos(angles), jnp.cos(angles)], axis=-1)
    sine_full = jnp.concatenate([jnp.sin(angles), jnp.sin(angles)], axis=-1)
    return (cosine_full, sine_full)


def rotate_half(values):
    half_size = values.shape[-1] // 2
    return jnp.concatenate([-values[..., half_size:], values[..., :half_size]], axis=-1)


def rotate(values, cosine_full, sine_full):
    return values * cosine_full[:, None, :] + rotate_half(values) * sine_full[:, None, :]


def rotate_back(values, cosine_full, sine_full):
    return values * cosine_full[:, None, :] - rotate_half(values) * sine_full[:, None, :]


def masked_scores(query_blk, key_col, allowed_rows):
    scores = jnp.einsum("qgd,kd->gqk", query_blk, key_col, preferred_element_type=jnp.float32)
    return jnp.where(allowed_rows[None], scores, -jnp.inf)


def per_device(tokens, doc_ids, norm_gains, w_qkv, b_qkv, w_out, w_gate, w_up, w_down, cotangent):
    n = lax.axis_size("dp")
    grid = Grid(n)
    A, T = grid.A, grid.T
    me = lax.axis_index("dp")
    line = me // T
    tok_rows, width = tokens.shape
    own, qkv = w_qkv.shape
    heads_all = width // HEAD_DIM
    kv_width = (qkv - width) // 2
    key_heads = kv_width // HEAD_DIM
    group = heads_all // key_heads
    ff_own = w_down.shape[0]
    ff_mine = A * ff_own
    bias_own = b_qkv.shape[0]
    pad = -(-(own + 3) // 16) * 16

    def at_columns(values, start, columns):
        return lax.dynamic_update_slice(jnp.zeros((columns,), BF), values, (start,))[None]

    packed = jnp.concatenate(
        [
            w_qkv,
            at_columns(b_qkv, me * bias_own, qkv),
            at_columns(norm_gains[0], me * own, qkv),
            at_columns(norm_gains[1], me * own, qkv),
            jnp.zeros((pad - own - 3, qkv), BF),
        ],
        axis=0,
    )
    packed_out = jnp.concatenate([w_out, jnp.zeros((pad - own, width), BF)], axis=0)
    qkv_full = gather_all(grid, packed).reshape(n * pad, qkv)
    out_full = gather_all(grid, packed_out).reshape(n * pad, width)

    def columns_of(weight):
        return weight.reshape(own, A, T, ff_own).transpose(2, 0, 1, 3).reshape(T, own, ff_mine)

    gate_up = jnp.stack([columns_of(w_gate), columns_of(w_up)], axis=1)
    gate_up = plane_exchange(grid, gate_up)
    gate_own = gate_up[:, 0].reshape(T * own, ff_mine)
    up_own = gate_up[:, 1].reshape(T * own, ff_mine)
    gate_weight = line_gather(grid, gate_own, line).reshape(width, ff_mine)
    up_weight = line_gather(grid, up_own, line).reshape(width, ff_mine)
    down_weight = line_gather(grid, w_down, line).reshape(ff_mine, width)
    cot_plane = plane_gather(grid, cotangent)

    spot = lax.broadcasted_iota(jnp.int32, (1, n * pad), 1)
    block, inner = spot // pad, spot % pad
    planes = len(grid.offsets)
    flip, rest = block // (planes * A), block % (planes * A)
    plane_off, line_off = rest // A, rest % A
    my_b, my_c, my_k = (me // (2 * grid.C)) % grid.B, (me // 2) % grid.C, me % 2
    src_b = (my_b - plane_off // grid.C) % grid.B
    src_c = (my_c - plane_off % grid.C) % grid.C
    src = (((line - line_off) % A * grid.B + src_b) * grid.C + src_c) * 2 + jnp.where(flip == 0, my_k, 1 - my_k)
    feature = jnp.where(inner < own, src * own + inner, -1)
    spread = (lax.broadcasted_iota(jnp.int32, (width, 1), 0) == feature).astype(BF)
    row_kind = lax.broadcasted_iota(jnp.int32, (8, 1), 0) + own + 1
    picked = dot((row_kind == inner).astype(BF), qkv_full)
    gain_first = picked[0, :width]
    gain_second = picked[1, :width]
    bias_column = (inner == own).astype(F32)

    cosine_full, sine_full = rope_tables(doc_ids, HEAD_DIM)
    row_ids = jnp.arange(tok_rows, dtype=jnp.int32)
    allowed = (doc_ids[:, None] == doc_ids[None, :]) & (row_ids[None, :] <= row_ids[:, None])
    resident = tokens.astype(F32)
    first_scale = lax.rsqrt(jnp.mean(resident * resident, axis=-1, keepdims=True) + NORM_EPS)
    first_plain = resident * first_scale
    normed_one = (first_plain * gain_first).astype(BF)
    normed_pad = (dot(normed_one, spread) + bias_column).astype(BF)
    projected = dot(normed_pad, qkv_full)
    queries = projected[:, :width].reshape(tok_rows, heads_all, HEAD_DIM)
    keys_raw = projected[:, width : width + kv_width].reshape(tok_rows, key_heads, HEAD_DIM)
    values_raw = projected[:, width + kv_width :].reshape(tok_rows, key_heads, HEAD_DIM)
    query_low = (
        (rotate(queries, cosine_full, sine_full) * 0.125)
        .astype(BF)
        .reshape(tok_rows, key_heads, group, HEAD_DIM)
    )
    key_low = rotate(keys_raw, cosine_full, sine_full).astype(BF)
    value_low = values_raw.astype(BF)
    head_outs = []
    head_logs = []
    for kv_index in range(key_heads):
        scores = masked_scores(query_low[:, kv_index], key_low[:, kv_index], allowed)
        row_max = jnp.max(scores, axis=-1, keepdims=True)
        exponent = jnp.exp(scores - row_max)
        row_total = jnp.sum(exponent, axis=-1, keepdims=True)
        prob_low = (exponent / row_total).astype(BF)
        head_outs.append(
            jnp.einsum("gqk,kd->qgd", prob_low, value_low[:, kv_index], preferred_element_type=F32)
        )
        head_logs.append(row_max + jnp.log(row_total))
    attended = jnp.stack(head_outs, axis=1).reshape(tok_rows, width).astype(BF)
    attended_pad = dot(attended, spread, out=BF)
    middle = resident + dot(attended_pad, out_full)
    second_scale = lax.rsqrt(jnp.mean(middle * middle, axis=-1, keepdims=True) + NORM_EPS)
    second_plain = middle * second_scale
    normed_two = (second_plain * gain_second).astype(BF)

    normed_plane = plane_gather(grid, normed_two)
    gate_val = dot(normed_plane, gate_weight)
    up_val = dot(normed_plane, up_weight)
    d_hidden = against(cot_plane, down_weight)
    sigmoid_gate = jax.nn.sigmoid(gate_val)
    activated = gate_val * sigmoid_gate
    hidden_act = (activated * up_val).astype(BF)
    d_gate = (d_hidden * up_val * sigmoid_gate * (1.0 + gate_val * (1.0 - sigmoid_gate))).astype(BF)
    d_up = (d_hidden * activated).astype(BF)
    d_normed_two = plane_scatter(grid, against(d_gate, gate_weight) + against(d_up, up_weight), tok_rows)
    out_part = plane_scatter(grid, dot(hidden_act, down_weight), tok_rows)
    activations = (middle + out_part).astype(BF)
    grad_gate = line_scatter(grid, rows_dot(normed_plane, d_gate).reshape(A, T * own, ff_mine), line)
    grad_up = line_scatter(grid, rows_dot(normed_plane, d_up).reshape(A, T * own, ff_mine), line)
    grad_down = line_scatter(grid, rows_dot(hidden_act, cot_plane).reshape(A, ff_own, width), line)
    both = jnp.stack(
        [grad_gate.astype(BF).reshape(T, own, ff_mine), grad_up.astype(BF).reshape(T, own, ff_mine)], axis=1
    )
    both = plane_exchange(grid, both)

    def columns_back(grad):
        return grad.reshape(T, own, A, ff_own).transpose(1, 2, 0, 3).reshape(own, A * T * ff_own).astype(F32)

    grad_gate = columns_back(both[:, 0])
    grad_up = columns_back(both[:, 1])

    upstream = cotangent.astype(F32)
    grad_gain_two = jnp.sum(d_normed_two * second_plain, axis=0)
    d_plain_two = d_normed_two * gain_second
    d_middle = upstream + second_scale * (
        d_plain_two - second_plain * jnp.mean(d_plain_two * second_plain, axis=-1, keepdims=True)
    )
    d_branch = d_middle.astype(BF)
    grad_out = scatter_all(grid, rows_dot(attended_pad, d_branch).reshape(n, pad, width))[:own]
    d_attended = against(against(d_branch, out_full).astype(BF), spread).astype(BF)
    d_attended = d_attended.reshape(tok_rows, key_heads, group, HEAD_DIM)
    key_grads = []
    value_grads = []
    query_grads = []
    for kv_index in range(key_heads):
        query_blk = query_low[:, kv_index]
        grad_blk = d_attended[:, kv_index]
        scores = masked_scores(query_blk, key_low[:, kv_index], allowed)
        prob_full = jnp.exp(scores - head_logs[kv_index])
        d_prob = jnp.einsum("qgd,kd->gqk", grad_blk, value_low[:, kv_index], preferred_element_type=F32)
        delta_row = jnp.sum(d_prob * prob_full, axis=-1, keepdims=True)
        d_score = (prob_full * (d_prob - delta_row)).astype(BF)
        value_grads.append(
            jnp.einsum("gqk,qgd->kd", prob_full.astype(BF), grad_blk, preferred_element_type=F32)
        )
        query_grads.append(
            jnp.einsum("gqk,kd->qgd", d_score, key_low[:, kv_index], preferred_element_type=F32)
        )
        key_grads.append(jnp.einsum("gqk,qgd->kd", d_score, query_blk, preferred_element_type=F32))
    d_query = jnp.stack(query_grads, axis=1).reshape(tok_rows, heads_all, HEAD_DIM)
    d_key = jnp.stack(key_grads, axis=1)
    d_value = jnp.stack(value_grads, axis=1)
    d_projected = jnp.concatenate(
        [
            (0.125 * rotate_back(d_query, cosine_full, sine_full)).reshape(tok_rows, width),
            rotate_back(d_key, cosine_full, sine_full).reshape(tok_rows, kv_width),
            d_value.reshape(tok_rows, kv_width),
        ],
        axis=-1,
    ).astype(BF)
    d_pad = against(d_projected, qkv_full)
    high = d_pad.astype(BF)
    low = (d_pad - high.astype(F32)).astype(BF)
    d_normed_one = against(high, spread) + against(low, spread)
    grad_gain_one = jnp.sum(d_normed_one * first_plain, axis=0)
    d_plain_one = d_normed_one * gain_first
    input_grad = d_middle + first_scale * (
        d_plain_one - first_plain * jnp.mean(d_plain_one * first_plain, axis=-1, keepdims=True)
    )
    grad_pad = rows_dot(normed_pad, d_projected).reshape(n, pad, qkv)
    row = lax.broadcasted_iota(jnp.int32, (1, pad, 1), 1)
    wide = ((0, qkv - width),)
    grad_pad = jnp.where(row == own + 1, jnp.pad(grad_gain_one, wide)[None, None], grad_pad)
    grad_pad = jnp.where(row == own + 2, jnp.pad(grad_gain_two, wide)[None, None], grad_pad)
    grad_pad = scatter_all(grid, grad_pad)
    grad_bias = lax.dynamic_slice(grad_pad[own], (me * bias_own,), (bias_own,))
    grad_gains = lax.dynamic_slice(grad_pad[own + 1 : own + 3], (0, me * own), (2, own))
    return (
        activations,
        input_grad,
        grad_gains,
        grad_pad[:own],
        grad_bias,
        grad_out,
        grad_gate,
        grad_up,
        grad_down,
    )


def solution(mesh):
    rows = P("dp", None)
    return jax.shard_map(
        per_device,
        mesh=mesh,
        in_specs=(rows, P("dp"), P(None, "dp"), rows, P("dp"), rows, rows, rows, rows, rows),
        out_specs=(rows, rows, P(None, "dp"), rows, P("dp"), rows, rows, rows, rows),
        check_vma=False,
    )
```
